32 devices in a mesh: req: 4 (over y, x), grp: 8 (over z, core).
Axes of the slice: x: 2, y: 2, z: 4, core: 2. Of those that a mesh axis runs over, the one named last changes fastest.
Arguments:
- item_table: bfloat16 [32768, 512], P('grp'), may hold values from -6 to 6
- cand_owner: int32 [4, 8192, 1], P('req', 'grp'), may hold values from 0 to 7; in each aligned block of 1024 rows (0 to 1023, 1024 to 2047, ..., all dimensions but the last counted through in order) at most 128 rows name the same one
- cand_row: int32 [4, 8192], P('req', 'grp'), may hold values from 0 to 4095
- hist_kv: bfloat16 [2, 4, 2048, 1024], P(None, 'req', 'grp'), may hold values from -6 to 6
- hist_len: int32 [4], P('req'), may hold values from 512 to 2048, as said below
- w_in: bfloat16 [2, 512, 1024], replicated, may hold values from -0.25 to 0.25
- w_out: bfloat16 [2, 512, 512], replicated, may hold values from -0.25 to 0.25
Outputs:
- candidate_states: bfloat16 [4, 8192, 512], P('req', 'grp')
The draws below stay inside these ranges and needn't reach their ends.
Inputs may be any that keep to these rules, and one draw needn't show every extreme that they name: `cand_owner`: among the 1024 candidates of one device, at most 128 name the same block, and some block is named exactly 128 times. `hist_len`: some request has all 2048 events live.
All inputs are finite; a program needn't handle non-finite values.
Results may differ from the reference program's by a relative error of at most 0.0085.
Values may be sent and summed in bfloat16 or wider, within the bound.
A program may use at most 128 MiB of HBM per device.

```python
import math
import jax
import jax.numpy as jnp
import numpy as np
from jax import lax

D = 512
HEADS = 4
HEAD = 128
LAYERS = 2
CAND_DEV = 1024
ITEMS_DEV = 4096
MOST = 128
REQS = 4
CAND = 8192
HIST = 2048
ITEMS = 32768
N_GRP = 8


def draw_hist_len(key, part):
    first_key, second_key = jax.random.split(jax.random.fold_in(key, 11))
    lengths = jax.random.randint(first_key, (REQS,), HIST // 4, HIST + 1)
    chosen = jax.random.randint(second_key, (), 0, REQS)
    return jnp.where(jnp.arange(REQS) == chosen, HIST, lengths).astype(jnp.int32)


def set_ends(entries, own_key, least, top_value):
    longest = entries.shape.index(max(entries.shape))
    spots = []
    for shift in (0, 1):
        where = [jax.random.randint(jax.random.fold_in(own_key, axis), (), 0, length) for axis, length in enumerate(entries.shape)]
        where[longest] = (where[longest] + shift) % entries.shape[longest]
        spots.append(tuple(where))
    return entries.at[spots[0]].set(least).at[spots[1]].set(top_value)


def block_levels(stream_key, dims, pieces, least, largest):
    level, own = 1.0, jax.random.fold_in(stream_key, 6)
    for axis_at, blocks in pieces:
        draws = jnp.exp(jax.random.uniform(jax.random.fold_in(own, axis_at), (blocks,), jnp.float32, least / len(pieces), largest / len(pieces)))
        level = level * jnp.repeat(draws, dims[axis_at] // blocks).reshape([-1 if axis == axis_at else 1 for axis in range(len(dims))])
    return level


def assign_block(own_key, own, number, rows, amount, top, most, lean):
    ranking = jax.random.permutation(own_key, amount)
    heavy_load, usual = shares(amount, rows * top, most, lean, True), shares(amount, rows * top, most, lean, False)
    places = jnp.arange(amount)

    def named(tallies, turn):
        used = int((tallies > 0).sum())
        fixed = max(1, used // 4)
        moved = fixed + (places - fixed + turn * (used - fixed)) % max(1, amount - fixed)
        return jnp.zeros((amount,), jnp.int32).at[ranking[jnp.where(places < fixed, places, moved)]].set(jnp.asarray(tallies, jnp.int32))

    tallies = jnp.where(number % 4 == 0, named(heavy_load, number // 4), named(usual, number - number // 4 - 1))
    mixed = jax.random.permutation(jax.random.fold_in(own, 3), amount)
    source_of, sink = mixed[0:amount // 2 * 2:2], mixed[1:amount // 2 * 2:2]
    slack = jnp.minimum(tallies[source_of] - 1, most - tallies[sink]) // 2
    slack = jnp.where((source_of == ranking[0]) | (sink == ranking[0]) | (tallies[sink] == 0), 0, jnp.maximum(slack, 0))
    moved = jax.random.randint(jax.random.fold_in(own, 4), (amount // 2,), 0, 1 << 20) % (slack + 1)
    tallies = tallies.at[source_of].add(-moved).at[sink].add(moved)
    labels = jnp.searchsorted(jnp.cumsum(tallies), jnp.arange(rows * top), side="right").astype(jnp.int32)
    listing = labels.reshape(top, rows).T
    listing = listing[jax.random.permutation(jax.random.fold_in(own, 1), rows)]
    turn = jax.random.randint(jax.random.fold_in(own, 2), (rows, 1), 0, top)
    return jnp.take_along_axis(listing, (jnp.arange(top)[None, :] + turn) % top, axis=1)


def shares(count, total, reach, skew, full):
    portions = [(1 << 20) // math.isqrt(rank ** skew) + 1 for rank in range(1, count + 1)]
    largest = reach if full else min(reach, max(-(-total // count), total * portions[0] // sum(portions)))
    least = 1 if total - largest >= count - 1 else 0
    holding, surplus = [largest] + [least] * (count - 1), total - largest - least * (count - 1)
    while surplus > 0:
        candidates = [i for i in range(1, count) if holding[i] < largest] or [i for i in range(1, count) if holding[i] < reach]
        whole, budget = sum([portions[i] for i in candidates]), surplus
        for i in candidates:
            extra = min(reach - holding[i], max(1, budget * portions[i] // whole), surplus)
            holding[i] = holding[i] + extra
            surplus = surplus - extra
    return np.array(holding)


def normal_values(stream_key, extent, width, limit, pieces=(), kind=jnp.bfloat16):
    drawn = jax.random.normal(stream_key, extent, jnp.float32) * width
    if len(pieces) > 0:
        drawn = block_levels(stream_key, extent, pieces, -0.22, 0.18) * drawn
    return jnp.clip(drawn, min=-limit, max=limit).astype(kind)


def setup_inputs(seed: int = 0) -> dict:
    keys = jax.random.split(jax.random.key(seed), 8)
    item_table = normal_values(keys[0], (ITEMS, D), 1.0, 6.0, ((0, 8),))
    cand_owner_keys = jax.random.split(jax.random.fold_in(keys[1], 1), REQS * CAND // CAND_DEV)
    cand_owner_turns = jax.random.permutation(jax.random.fold_in(keys[1], 3), REQS * CAND // CAND_DEV)
    cand_owner = jax.vmap(lambda own, number: assign_block(jax.random.fold_in(keys[1], 2), own, number, CAND_DEV, N_GRP, 1, MOST, 2))(cand_owner_keys, cand_owner_turns).reshape((REQS, CAND, 1))
    cand_row = set_ends(jax.random.randint(keys[2], (REQS, CAND), 0, ITEMS_DEV), jax.random.fold_in(keys[2], 1), 0, ITEMS_DEV - 1).astype(jnp.int32)
    hist_kv = normal_values(keys[3], (LAYERS, REQS, HIST, 2 * D), 1.0, 6.0, ((1, 4), (2, 8)))
    hist_len = draw_hist_len(jax.random.fold_in(keys[7], 71), 0)
    w_in = normal_values(keys[5], (LAYERS, D, 2 * D), D ** -0.5, 0.25)
    w_out = normal_values(keys[6], (LAYERS, D, D), D ** -0.5, 0.25)
    return {"item_table": item_table, "cand_owner": cand_owner, "cand_row": cand_row, "hist_kv": hist_kv, "hist_len": hist_len, "w_in": w_in, "w_out": w_out}


score_scale = 0.35
epsilon = 1e-05

def normalize(values):
    center = values - lax.optimization_barrier(jnp.mean(values, axis=-1, keepdims=True))
    return center * lax.rsqrt(lax.optimization_barrier(jnp.mean(center * center, axis=-1, keepdims=True)) + epsilon)

def ref_layer(rows_now, cache_rows, length, weight_in, weight_out):
    normed = normalize(rows_now.astype(jnp.float32)).astype(jnp.bfloat16)
    projected = jax.nn.silu(jnp.dot(normed, weight_in, preferred_element_type=jnp.float32))
    gate_vals = projected[:, :D]
    queries = projected[:, D:].astype(jnp.bfloat16)
    key_rows = cache_rows[:, :D].reshape(HIST, HEADS, HEAD).astype(jnp.float32)
    value_rows = cache_rows[:, D:].reshape(HIST, HEADS, HEAD).astype(jnp.float32)
    live = jnp.arange(HIST, dtype=jnp.int32) < length
    block_rows = math.gcd(CAND, 1024)
    blocks = queries.reshape(CAND // block_rows, block_rows, HEADS, HEAD)

    def one_block(query_block):
        scores = jnp.einsum('chd,khd->hck', query_block.astype(jnp.float32), key_rows) * score_scale
        weights = jnp.where(live[None, None, :], jax.nn.silu(scores), 0.0).astype(jnp.bfloat16)
        attended = jnp.einsum('hck,khd->chd', weights.astype(jnp.float32), value_rows)
        return attended.reshape(block_rows, D)
    attended = lax.map(one_block, blocks).reshape(CAND, D)
    hidden = (normalize(attended) * gate_vals).astype(jnp.bfloat16)
    return (rows_now.astype(jnp.float32) + jnp.dot(hidden, weight_out, preferred_element_type=jnp.float32)).astype(jnp.bfloat16)

def reference(item_table, cand_owner, cand_row, hist_kv, hist_len, w_in, w_out):
    item_ids = (cand_owner[:, :, 0] * ITEMS_DEV + cand_row).astype(jnp.int32)
    outputs = []
    for request in range(REQS):
        rows_now = jnp.take(item_table, item_ids[request], axis=0)
        for layer_index in range(LAYERS):
            rows_now = ref_layer(rows_now, hist_kv[layer_index, request], hist_len[request], w_in[layer_index], w_out[layer_index])
        outputs.append(rows_now)
    return jnp.stack(outputs)
```

```python
from functools import partial

import jax
import jax.numpy as jnp
from jax import lax
from jax.experimental import pallas as pl
from jax.experimental.pallas import tpu as pltpu
from jax.sharding import PartitionSpec as P

D = 512
HEADS = 4
HEAD = 128
LAYERS = 2
MOST = 128
PARTS = 1
MESH = pl.DeviceIdType.MESH

score_scale = 0.35
epsilon = 1e-05


def normalize(values):
    center = values - jnp.mean(values, axis=-1, keepdims=True)
    return center * lax.rsqrt(jnp.mean(center * center, axis=-1, keepdims=True) + epsilon)


def silu_of_twice(half):
    return half + half * jnp.tanh(half)


def kernel(
    groups,
    len_ref, owner_ref, row_ref, table_hbm, hist_ref, w_in_hbm, w_out_hbm, out_ref,
    table_ref, w_in_ref, w_out_ref, kv, live_values, place, asked, wanted, found, handed, returned, queries, gate, summed,
    load_sem, own_sem, z_recv, s_recv, r_send, l_send, s_send, ask_send, ask_recv,
    hand_send, hand_recv, back_send, back_recv,
):
    chips = groups // 2
    me = lax.axis_index("grp")
    pos, core = me // 2, me % 2
    sibling = 2 * pos + 1 - core
    lower = pos < chips // 2
    inner = jnp.logical_and(pos > 0, pos + 1 < chips)
    helper = jnp.logical_or(pos == 1, pos == chips - 2)
    inward = jnp.where(lower, 1, -1)
    end_device = 2 * jnp.where(lower, 0, chips - 1) + core
    cands = row_ref.shape[1]
    items = table_ref.shape[0]
    hist_rows = hist_ref.shape[1]
    keys_all = groups * hist_rows
    tile = 2 * MOST
    slots = groups * MOST
    half = hist_rows // PARTS
    f32, bf16 = jnp.float32, jnp.bfloat16

    barrier = pltpu.get_barrier_semaphore()

    @pl.loop(1, groups)
    def _(k):
        pl.semaphore_signal(
            barrier, inc=1, device_id={"grp": (me + k) % groups}, device_id_type=MESH
        )

    own_copies = [
        pltpu.make_async_copy(hist_ref.at[layer], kv.at[layer, me], own_sem.at[layer])
        for layer in range(LAYERS)
    ]
    loads = [
        pltpu.make_async_copy(far, near, load_sem.at[index])
        for index, (far, near) in enumerate(
            [(table_hbm, table_ref), (w_in_hbm, w_in_ref), (w_out_hbm, w_out_ref)]
        )
    ]
    for copy in own_copies + loads:
        copy.start()
    pl.semaphore_wait(barrier, groups - 1)

    def push(layer, chip, lane, part, target, send, recv):
        block = kv.at[layer, 2 * chip + lane, pl.ds(part * half, half)]
        return pltpu.make_async_remote_copy(
            src_ref=block, dst_ref=block, send_sem=send.at[layer, chip, part],
            recv_sem=recv.at[layer, chip, part], device_id={"grp": target}, device_id_type=MESH,
        )

    def to_right(layer, chip, part):
        return push(layer, chip, core, part, me + 2, r_send, z_recv)

    def to_left(layer, chip, part):
        return push(layer, chip, core, part, me - 2, l_send, z_recv)

    def to_sibling(layer, chip, part):
        return push(layer, chip, core, part, sibling, s_send, s_recv)

    def from_sibling(layer, chip, part):
        return push(layer, chip, 1 - core, part, sibling, s_send, s_recv)

    def margin(layer):
        return 1 if layer == 0 else 0

    def goes_right(layer, chip):
        return jnp.logical_and(chip <= pos, pos + 1 < chips - margin(layer))

    def goes_left(layer, chip):
        return jnp.logical_and(chip >= pos, pos > margin(layer))

    def goes_across(layer):
        return inner if layer == 0 else pos >= 0

    def pass_on(layer, chip, inside=True, outside=True, across=True):
        for part in range(PARTS):
            if inside or outside:
                right = goes_right(layer, chip)
                left = goes_left(layer, chip)
                if not outside:
                    right, left = jnp.logical_and(right, lower), jnp.logical_and(left, jnp.logical_not(lower))
                if not inside:
                    right, left = jnp.logical_and(right, jnp.logical_not(lower)), jnp.logical_and(left, lower)

                @pl.when(right)
                def _():
                    to_right(layer, chip, part).start()

                @pl.when(left)
                def _():
                    to_left(layer, chip, part).start()

            if across:
                @pl.when(goes_across(layer))
                def _():
                    to_sibling(layer, chip, part).start()

    def when_there(chip, act):
        @pl.when(jnp.logical_and(chip >= 0, chip < chips))
        def _():
            act(chip)

    def relay(layer, chip):
        def act(chip):
            for part in range(PARTS):
                to_right(layer, chip, part).wait_recv()
            pass_on(layer, chip)

        when_there(chip, act)

    own_copies[0].wait()
    pass_on(0, pos)
    own_copies[1].wait()
    pass_on(1, pos, inside=False)

    owners = jnp.concatenate(
        [
            jnp.broadcast_to(owner_ref[:, start : start + 128].astype(f32), (128, 128)).T[:, 0:1]
            for start in range(0, cands, 128)
        ],
        axis=0,
    ).astype(jnp.int32)
    names = (owners == lax.broadcasted_iota(jnp.int32, (cands, 128), 1)).astype(f32)
    names16 = names.astype(bf16)
    item_rows = row_ref[...]
    high = (item_rows >> 6).astype(f32)
    low = (item_rows & 63).astype(f32)
    halves = jnp.concatenate([high, low, jnp.zeros((6, cands), f32)], axis=0).astype(bf16)
    listed = jnp.zeros((8, slots), f32)
    for start in range(0, cands, tile):
        earlier = (
            lax.broadcasted_iota(jnp.int32, (tile, cands), 1)
            < start + lax.broadcasted_iota(jnp.int32, (tile, cands), 0)
        ).astype(f32).astype(bf16)
        rank = jnp.dot(earlier, names16, preferred_element_type=f32)
        own_rank = jnp.sum(rank * names[start : start + tile], axis=1, keepdims=True)
        flat = owners[start : start + tile] * MOST + own_rank.astype(jnp.int32)
        chosen = (
            (flat == lax.broadcasted_iota(jnp.int32, (tile, slots), 1)).astype(f32).astype(bf16)
        )
        listed += jnp.dot(halves[:, start : start + tile], chosen, preferred_element_type=f32)
        for chip in range(chips):
            place[chip, start : start + tile, :] = chosen[:, chip * tile : (chip + 1) * tile]
    requested = (listed[0:1] * 64.0 + listed[1:2]).astype(jnp.int32)
    for owner in range(groups):
        asked[owner] = requested[:, owner * MOST : (owner + 1) * MOST]

    def ask(peer, slot):
        return pltpu.make_async_remote_copy(
            src_ref=asked.at[peer], dst_ref=wanted.at[slot], send_sem=ask_send.at[peer],
            recv_sem=ask_recv.at[slot], device_id={"grp": peer}, device_id_type=MESH,
        )

    @pl.loop(1, groups)
    def _(k):
        ask((me + k) % groups, me).start()

    wanted[me] = asked[me]

    @pl.loop(1, groups)
    def _(k):
        peer = (me + k) % groups
        ask(peer, peer).wait_recv()

    at_once = 4
    chunk = 512
    batches = groups // at_once

    def batch_at(turn):
        return jnp.where(lower, batches - 1 - turn, turn)

    def hand_over(turn):
        block = pl.ds(batch_at(turn) * at_once, at_once)
        target = 2 * jnp.clip(pos, 1, chips - 2) + core
        return pltpu.make_async_remote_copy(
            src_ref=found.at[block], dst_ref=handed.at[block], send_sem=hand_send.at[turn],
            recv_sem=hand_recv.at[turn], device_id={"grp": target}, device_id_type=MESH,
        )

    def handed_over(turn):
        block = pl.ds(batch_at(turn) * at_once, at_once)
        return pltpu.make_async_remote_copy(
            src_ref=found.at[block], dst_ref=handed.at[block], send_sem=hand_send.at[turn],
            recv_sem=hand_recv.at[turn], device_id={"grp": end_device}, device_id_type=MESH,
        )

    def gather(turn):
        batch = batch_at(turn)
        columns = []
        for k in range(at_once):
            line = wanted[batch * at_once + k].astype(f32)
            columns.append(jnp.broadcast_to(line, (MOST, MOST)).T[:, 0:1].astype(jnp.int32))
        column = jnp.concatenate(columns, axis=0)
        total = jnp.zeros((at_once * MOST, D), f32)
        for start in range(0, items, chunk):
            picks = (
                column
                == start + lax.broadcasted_iota(jnp.int32, (at_once * MOST, chunk), 1)
            ).astype(f32).astype(bf16)
            total += jnp.dot(
                picks, table_ref[start : start + chunk, :], preferred_element_type=f32
            )
        found[pl.ds(batch * at_once, at_once)] = total.astype(bf16).reshape(at_once, MOST, D)

        @pl.when(jnp.logical_not(inner))
        def _():
            hand_over(turn).start()

    loads[0].wait()
    pl.loop(0, batches)(gather)
    loads[1].wait()
    loads[2].wait()

    def rows_of(start, size=tile):
        return pl.ds(pl.multiple_of(start, tile), size)

    def project(layer, start, rows):
        normed = normalize(rows.astype(f32)).astype(bf16)
        projected = silu_of_twice(
            0.5 * jnp.dot(normed, w_in_ref[layer], preferred_element_type=f32)
        )
        gate[rows_of(start), :] = projected[:, :D]
        queries[rows_of(start), :] = projected[:, D:].astype(bf16)
        summed[rows_of(start), :] = jnp.zeros((tile, D), f32)

    length = len_ref[0]

    def open_values(layer, chip):
        for part in range(PARTS):
            from_sibling(layer, chip, part).wait_recv()
        for lane in range(2):
            first = (2 * chip + lane) * hist_rows
            position = first + lax.broadcasted_iota(jnp.int32, (hist_rows, D), 0)
            values = kv[layer, 2 * chip + lane, :, D:].astype(f32)
            live_values[pl.ds(pl.multiple_of(first, hist_rows), hist_rows), :] = jnp.where(
                position < length, values, 0.0
            ).astype(bf16)

    def weigh(asking, keys):
        scores = lax.dot_general(
            asking, keys, (((1,), (1,)), ((), ())), preferred_element_type=f32
        )
        return silu_of_twice((scores * (0.5 * score_scale)).astype(bf16))

    def attend(layer, chip, size, block):
        open_values(layer, chip)
        here = pl.ds(pl.multiple_of(2 * chip * hist_rows, 2 * hist_rows), 2 * hist_rows)

        @pl.loop(0, size // block)
        def _(step):
            rows = rows_of(step * block, block)
            for head in range(HEADS):
                cols = slice(head * HEAD, (head + 1) * HEAD)
                keys = kv[layer, pl.ds(2 * chip, 2), :, cols].reshape(2 * hist_rows, HEAD)
                summed[rows, cols] += jnp.dot(
                    weigh(queries[rows, cols], keys), live_values[here, cols],
                    preferred_element_type=f32,
                )

    def attend_in_turn(layer, size, block):
        @pl.loop(0, 2 * chips - 1)
        def _(turn):
            distance = (turn + 1) // 2
            chip = pos + inward * jnp.where(turn % 2 == 0, distance, -distance)

            @pl.when(distance > 1)
            def _():
                relay(layer, chip)

            when_there(chip, lambda chip: attend(layer, chip, size, block))

    def attend_all(layer, start):
        rows = rows_of(start)
        span = min(2048, keys_all)
        lanes = span // hist_rows
        for head in range(HEADS):
            cols = slice(head * HEAD, (head + 1) * HEAD)
            total = None
            for first in range(0, keys_all, span):
                keys = kv[
                    layer, first // hist_rows : first // hist_rows + lanes, :, cols
                ].reshape(span, HEAD)
                part = jnp.dot(
                    weigh(queries[rows, cols], keys), live_values[first : first + span, cols],
                    preferred_element_type=f32,
                )
                total = part if total is None else total + part
            summed[rows, cols] = total

    def finish(layer, start, rows):
        here = rows_of(start)
        hidden = (normalize(summed[here, :]) * gate[here, :]).astype(bf16)
        return (
            rows.astype(f32)
            + jnp.dot(hidden, w_out_ref[layer], preferred_element_type=f32)
        ).astype(bf16)

    def pair(rows_ref, chip):
        return rows_ref[pl.ds(2 * chip, 2)].reshape(tile, D)

    def give_back(source, owner, which, peer):
        return pltpu.make_async_remote_copy(
            src_ref=source.at[peer], dst_ref=returned.at[owner], send_sem=back_send.at[which, peer],
            recv_sem=back_recv.at[owner], device_id={"grp": peer}, device_id_type=MESH,
        )

    def send_home(source, owner, which, chip):
        source[pl.ds(2 * chip, 2)] = finish(0, chip * tile, pair(source, chip)).reshape(2, MOST, D)

        @pl.loop(0, 2)
        def _(lane):
            peer = 2 * chip + lane

            @pl.when(peer != me)
            def _():
                give_back(source, owner, which, peer).start()

            @pl.when(peer == me)
            def _():
                returned[owner] = source[peer]

    def home_at(turn):
        return jnp.where(lower, chips - 1 - turn, turn)

    @pl.when(inner)
    def _():
        @pl.loop(0, chips)
        def _(chip):
            project(0, chip * tile, pair(found, chip))

        relay(0, pos - inward)
        relay(0, pos + inward)
        pass_on(1, pos, outside=False, across=False)
        attend_in_turn(0, slots, min(slots, 1024))

        @pl.loop(0, chips)
        def _(turn):
            send_home(found, me, 0, home_at(turn))

    @pl.when(jnp.logical_not(inner))
    def _():
        hand_over(0).wait_send()
        pass_on(1, pos, outside=False, across=False)

    @pl.loop(0, batches)
    def _(turn):
        @pl.when(helper)
        def _():
            handed_over(turn).wait_recv()

            @pl.loop(0, at_once // 2)
            def _(k):
                chip = batch_at(turn) * (at_once // 2) + k
                project(0, chip * tile, pair(handed, chip))
                attend_all(0, chip * tile)
                send_home(handed, end_device, 1, chip)

        @pl.when(turn == 0)
        def _():
            relay(1, pos + inward)

    relay(1, pos - inward)

    def owner_at(turn):
        first = chips // 2
        chip = jnp.where(turn < first, (turn + 1) % first, turn)
        return jnp.where(lower, chip, chips - 1 - chip)

    def enter(turn):
        chip = owner_at(turn)
        worker = 2 * jnp.clip(chip, 1, chips - 2)

        @pl.loop(0, 2)
        def _(lane):
            @pl.when(worker + lane != me)
            def _():
                give_back(returned, 2 * chip + lane, 0, worker + lane).wait_recv()

        project(1, turn * tile, pair(returned, chip))

    def leave(turn, fresh=False):
        chip = owner_at(turn)
        rows = finish(1, turn * tile, pair(returned, chip))
        moved = jnp.dot(place[chip], rows, preferred_element_type=f32).astype(bf16)
        out_ref[...] = moved if fresh else out_ref[...] + moved

    near = chips // 2
    pl.loop(0, near)(enter)
    attend_in_turn(1, near * tile, min(near * tile, 512))
    leave(0, fresh=True)
    pl.loop(1, near)(leave)

    @pl.loop(near, chips)
    def _(turn):
        enter(turn)
        attend_all(1, turn * tile)
        leave(turn)

    for layer in range(LAYERS):
        @pl.loop(0, chips)
        def _(chip):
            for part in range(PARTS):
                @pl.when(goes_right(layer, chip))
                def _():
                    to_right(layer, chip, part).wait_send()

                @pl.when(goes_left(layer, chip))
                def _():
                    to_left(layer, chip, part).wait_send()

                @pl.when(goes_across(layer))
                def _():
                    to_sibling(layer, chip, part).wait_send()

    @pl.loop(1, groups)
    def _(k):
        peer = (me + k) % groups
        ask(peer, peer).wait_send()

        @pl.when(inner)
        def _():
            give_back(found, me, 0, peer).wait_send()

        @pl.when(helper)
        def _():
            give_back(handed, end_device, 1, peer).wait_send()

    @pl.when(jnp.logical_not(inner))
    def _():
        @pl.loop(1, batches)
        def _(turn):
            hand_over(turn).wait_send()


def body(item_table, cand_owner, cand_row, hist_kv, hist_len, w_in, w_out):
    groups = lax.axis_size("grp")
    cands = cand_row.shape[1]
    hist_rows = hist_kv.shape[2]
    vmem = pl.BlockSpec(memory_space=pltpu.VMEM)
    far = pl.BlockSpec(memory_space=pl.ANY)
    dma, f32, bf16 = pltpu.SemaphoreType.DMA, jnp.float32, jnp.bfloat16
    chips = groups // 2
    rows = pl.pallas_call(
        partial(kernel, groups),
        out_shape=jax.ShapeDtypeStruct((cands, D), bf16),
        in_specs=[
            pl.BlockSpec(memory_space=pltpu.SMEM), vmem, vmem, far, far, far, far,
        ],
        out_specs=vmem,
        scratch_shapes=[
            pltpu.VMEM(item_table.shape, bf16),
            pltpu.VMEM(w_in.shape, bf16),
            pltpu.VMEM(w_out.shape, bf16),
            pltpu.VMEM((LAYERS, groups, hist_rows, 2 * D), bf16),
            pltpu.VMEM((groups * hist_rows, D), bf16),
            pltpu.VMEM((chips, cands, 2 * MOST), bf16),
            pltpu.VMEM((groups, 1, MOST), jnp.int32),
            pltpu.VMEM((groups, 1, MOST), jnp.int32),
            pltpu.VMEM((groups, MOST, D), bf16),
            pltpu.VMEM((groups, MOST, D), bf16),
            pltpu.VMEM((groups, MOST, D), bf16),
            pltpu.VMEM((groups * MOST, D), bf16),
            pltpu.VMEM((groups * MOST, D), f32),
            pltpu.VMEM((groups * MOST, D), f32),
            dma((3,)),
            dma((LAYERS,)),
            dma((LAYERS, chips, PARTS)),
            dma((LAYERS, chips, PARTS)),
            dma((LAYERS, chips, PARTS)),
            dma((LAYERS, chips, PARTS)),
            dma((LAYERS, chips, PARTS)),
            dma((groups,)),
            dma((groups,)),
            dma((groups // 4,)),
            dma((groups // 4,)),
            dma((2, groups)),
            dma((groups,)),
        ],
        compiler_params=pltpu.CompilerParams(
            collective_id=0, has_side_effects=True, vmem_limit_bytes=56 * 1024 * 1024
        ),
    )(hist_len, cand_owner[:, :, 0], cand_row, item_table, hist_kv[:, 0], w_in, w_out)
    return rows[None]


def solution(mesh):
    in_specs = (
        P("grp", None),
        P("req", "grp", None),
        P("req", "grp"),
        P(None, "req", "grp", None),
        P("req"),
        P(),
        P(),
    )
    out_specs = P("req", "grp", None)
    return jax.shard_map(body, mesh=mesh, in_specs=in_specs, out_specs=out_specs, check_vma=False)
```

```python
from functools import partial

import jax
import jax.numpy as jnp
from jax import lax
from jax.experimental import pallas as pl
from jax.experimental.pallas import tpu as pltpu
from jax.sharding import PartitionSpec as P

D = 512
HEADS = 4
HEAD = 128
LAYERS = 2
MOST = 128
PARTS = 2
MESH = pl.DeviceIdType.MESH

score_scale = 0.35
epsilon = 1e-05


def normalize(values):
    center = values - jnp.mean(values, axis=-1, keepdims=True)
    return center * lax.rsqrt(jnp.mean(center * center, axis=-1, keepdims=True) + epsilon)


def silu_of_twice(half):
    return half + half * jnp.tanh(half)


def kernel(
    groups,
    len_ref, owner_ref, row_ref, table_hbm, hist_ref, w_in_hbm, w_out_hbm, out_ref,
    table_ref, w_in_ref, w_out_ref, kv, live_values, place, asked, wanted, found, handed, returned, queries, gate, summed,
    load_sem, own_sem, z_recv, s_recv, r_send, l_send, s_send, ask_send, ask_recv,
    hand_send, hand_recv, back_send, back_recv,
):
    chips = groups // 2
    me = lax.axis_index("grp")
    pos, core = me // 2, me % 2
    sibling = 2 * pos + 1 - core
    lower = pos < chips // 2
    inner = jnp.logical_and(pos > 0, pos + 1 < chips)
    helper = jnp.logical_or(pos == 1, pos == chips - 2)
    inward = jnp.where(lower, 1, -1)
    end_device = 2 * jnp.where(lower, 0, chips - 1) + core
    cands = row_ref.shape[1]
    items = table_ref.shape[0]
    hist_rows = hist_ref.shape[1]
    keys_all = groups * hist_rows
    tile = 2 * MOST
    slots = groups * MOST
    half = hist_rows // PARTS
    f32, bf16 = jnp.float32, jnp.bfloat16

    barrier = pltpu.get_barrier_semaphore()

    @pl.loop(1, groups)
    def _(k):
        pl.semaphore_signal(
            barrier, inc=1, device_id={"grp": (me + k) % groups}, device_id_type=MESH
        )

    own_copies = [
        pltpu.make_async_copy(hist_ref.at[layer], kv.at[layer, me], own_sem.at[layer])
        for layer in range(LAYERS)
    ]
    loads = [
        pltpu.make_async_copy(far, near, load_sem.at[index])
        for index, (far, near) in enumerate(
            [(table_hbm, table_ref), (w_in_hbm, w_in_ref), (w_out_hbm, w_out_ref)]
        )
    ]
    for copy in own_copies + loads:
        copy.start()

    def push(layer, chip, lane, part, target, send, recv):
        block = kv.at[layer, 2 * chip + lane, pl.ds(part * half, half)]
        return pltpu.make_async_remote_copy(
            src_ref=block, dst_ref=block, send_sem=send.at[layer, chip, part],
            recv_sem=recv.at[layer, chip, part], device_id={"grp": target}, device_id_type=MESH,
        )

    def to_right(layer, chip, part):
        return push(layer, chip, core, part, me + 2, r_send, z_recv)

    def to_left(layer, chip, part):
        return push(layer, chip, core, part, me - 2, l_send, z_recv)

    def to_sibling(layer, chip, part):
        return push(layer, chip, core, part, sibling, s_send, s_recv)

    def from_sibling(layer, chip, part):
        return push(layer, chip, 1 - core, part, sibling, s_send, s_recv)

    def margin(layer):
        return 1 if layer == 0 else 0

    def goes_right(layer, chip):
        return jnp.logical_and(chip <= pos, pos + 1 < chips - margin(layer))

    def goes_left(layer, chip):
        return jnp.logical_and(chip >= pos, pos > margin(layer))

    def goes_across(layer):
        return inner if layer == 0 else pos >= 0

    def pass_on(layer, chip, inside=True, outside=True, across=True, parts=range(PARTS)):
        for part in parts:
            if inside or outside:
                right = goes_right(layer, chip)
                left = goes_left(layer, chip)
                if not outside:
                    right, left = jnp.logical_and(right, lower), jnp.logical_and(left, jnp.logical_not(lower))
                if not inside:
                    right, left = jnp.logical_and(right, jnp.logical_not(lower)), jnp.logical_and(left, lower)

                @pl.when(right)
                def _():
                    to_right(layer, chip, part).start()

                @pl.when(left)
                def _():
                    to_left(layer, chip, part).start()

            if across:
                @pl.when(goes_across(layer))
                def _():
                    to_sibling(layer, chip, part).start()

    def when_there(chip, act):
        @pl.when(jnp.logical_and(chip >= 0, chip < chips))
        def _():
            act(chip)

    def relay(layer, chip, parts=range(PARTS)):
        def act(chip):
            for part in parts:
                to_right(layer, chip, part).wait_recv()
                pass_on(layer, chip, parts=[part])

        when_there(chip, act)

    owners = jnp.concatenate(
        [
            jnp.broadcast_to(owner_ref[:, start : start + 128].astype(f32), (128, 128)).T[:, 0:1]
            for start in range(0, cands, 128)
        ],
        axis=0,
    ).astype(jnp.int32)
    names = (owners == lax.broadcasted_iota(jnp.int32, (cands, 128), 1)).astype(f32)
    names16 = names.astype(bf16)
    item_rows = row_ref[...]
    high = (item_rows >> 6).astype(f32)
    low = (item_rows & 63).astype(f32)
    halves = jnp.concatenate([high, low, jnp.zeros((6, cands), f32)], axis=0).astype(bf16)
    listed = jnp.zeros((8, slots), f32)
    for start in range(0, cands, tile):
        earlier = (
            lax.broadcasted_iota(jnp.int32, (tile, cands), 1)
            < start + lax.broadcasted_iota(jnp.int32, (tile, cands), 0)
        ).astype(f32).astype(bf16)
        rank = jnp.dot(earlier, names16, preferred_element_type=f32)
        own_rank = jnp.sum(rank * names[start : start + tile], axis=1, keepdims=True)
        flat = owners[start : start + tile] * MOST + own_rank.astype(jnp.int32)
        chosen = (
            (flat == lax.broadcasted_iota(jnp.int32, (tile, slots), 1)).astype(f32).astype(bf16)
        )
        listed += jnp.dot(halves[:, start : start + tile], chosen, preferred_element_type=f32)
        for chip in range(chips):
            place[chip, start : start + tile, :] = chosen[:, chip * tile : (chip + 1) * tile]
    requested = (listed[0:1] * 64.0 + listed[1:2]).astype(jnp.int32)
    for owner in range(groups):
        asked[owner] = requested[:, owner * MOST : (owner + 1) * MOST]

    pl.semaphore_wait(barrier, groups - 1)

    def ask(peer, slot):
        return pltpu.make_async_remote_copy(
            src_ref=asked.at[peer], dst_ref=wanted.at[slot], send_sem=ask_send.at[peer],
            recv_sem=ask_recv.at[slot], device_id={"grp": peer}, device_id_type=MESH,
        )

    @pl.loop(1, groups)
    def _(k):
        ask((me + k) % groups, me).start()

    own_copies[0].wait()
    pass_on(0, pos)
    own_copies[1].wait()

    @pl.when(inner)
    def _():
        pass_on(1, pos, inside=False)

    @pl.when(jnp.logical_not(inner))
    def _():
        pass_on(1, pos)

    wanted[me] = asked[me]

    @pl.loop(1, groups)
    def _(k):
        peer = (me + k) % groups
        ask(peer, peer).wait_recv()

    early, late = range(PARTS // 2), range(PARTS // 2, PARTS)

    @pl.when(inner)
    def _():
        relay(0, pos - inward, early)

    at_once = 4
    chunk = 512
    batches = groups // at_once

    def batch_at(turn):
        return jnp.where(lower, batches - 1 - turn, turn)

    def hand_over(turn):
        block = pl.ds(batch_at(turn) * at_once, at_once)
        target = 2 * jnp.clip(pos, 1, chips - 2) + core
        return pltpu.make_async_remote_copy(
            src_ref=found.at[block], dst_ref=handed.at[block], send_sem=hand_send.at[turn],
            recv_sem=hand_recv.at[turn], device_id={"grp": target}, device_id_type=MESH,
        )

    def handed_over(turn):
        block = pl.ds(batch_at(turn) * at_once, at_once)
        return pltpu.make_async_remote_copy(
            src_ref=found.at[block], dst_ref=handed.at[block], send_sem=hand_send.at[turn],
            recv_sem=hand_recv.at[turn], device_id={"grp": end_device}, device_id_type=MESH,
        )

    def gather(turn):
        batch = batch_at(turn)
        columns = []
        for k in range(at_once):
            line = wanted[batch * at_once + k].astype(f32)
            columns.append(jnp.broadcast_to(line, (MOST, MOST)).T[:, 0:1].astype(jnp.int32))
        column = jnp.concatenate(columns, axis=0)
        total = jnp.zeros((at_once * MOST, D), f32)
        for start in range(0, items, chunk):
            picks = (
                column
                == start + lax.broadcasted_iota(jnp.int32, (at_once * MOST, chunk), 1)
            ).astype(f32).astype(bf16)
            total += jnp.dot(
                picks, table_ref[start : start + chunk, :], preferred_element_type=f32
            )
        found[pl.ds(batch * at_once, at_once)] = total.astype(bf16).reshape(at_once, MOST, D)

        @pl.when(jnp.logical_not(inner))
        def _():
            hand_over(turn).start()

        @pl.when(jnp.logical_and(inner, turn == 0))
        def _():
            relay(0, pos - inward, late)
            pass_on(1, pos, outside=False, across=False)

    loads[0].wait()
    pl.loop(0, batches)(gather)
    loads[1].wait()
    loads[2].wait()

    def rows_of(start, size=tile):
        return pl.ds(pl.multiple_of(start, tile), size)

    def project(layer, start, rows):
        normed = normalize(rows.astype(f32)).astype(bf16)
        projected = silu_of_twice(
            0.5 * jnp.dot(normed, w_in_ref[layer], preferred_element_type=f32)
        )
        gate[rows_of(start), :] = projected[:, :D]
        queries[rows_of(start), :] = projected[:, D:].astype(bf16)
        summed[rows_of(start), :] = jnp.zeros((tile, D), f32)

    length = len_ref[0]

    def open_values(layer, chip):
        for part in range(PARTS):
            from_sibling(layer, chip, part).wait_recv()
        for lane in range(2):
            first = (2 * chip + lane) * hist_rows
            position = first + lax.broadcasted_iota(jnp.int32, (hist_rows, D), 0)
            values = kv[layer, 2 * chip + lane, :, D:].astype(f32)
            live_values[pl.ds(pl.multiple_of(first, hist_rows), hist_rows), :] = jnp.where(
                position < length, values, 0.0
            ).astype(bf16)

    def weigh(asking, keys):
        scores = lax.dot_general(
            asking, keys, (((1,), (1,)), ((), ())), preferred_element_type=f32
        )
        return silu_of_twice((scores * (0.5 * score_scale)).astype(bf16))

    def attend(layer, chip, size, block):
        open_values(layer, chip)
        here = pl.ds(pl.multiple_of(2 * chip * hist_rows, 2 * hist_rows), 2 * hist_rows)

        @pl.loop(0, size // block)
        def _(step):
            rows = rows_of(step * block, block)
            for head in range(HEADS):
                cols = slice(head * HEAD, (head + 1) * HEAD)
                keys = kv[layer, pl.ds(2 * chip, 2), :, cols].reshape(2 * hist_rows, HEAD)
                summed[rows, cols] += jnp.dot(
                    weigh(queries[rows, cols], keys), live_values[here, cols],
                    preferred_element_type=f32,
                )

    def attend_in_turn(layer, size, block):
        @pl.loop(0, 2 * chips - 1)
        def _(turn):
            distance = (turn + 1) // 2
            chip = pos + inward * jnp.where(turn % 2 == 0, distance, -distance)

            @pl.when(distance > 1)
            def _():
                relay(layer, chip)

            when_there(chip, lambda chip: attend(layer, chip, size, block))

    def attend_all(layer, start, first=0, count=groups, more=False):
        rows = rows_of(start)
        most = max(1, 2048 // hist_rows)
        for head in range(HEADS):
            cols = slice(head * HEAD, (head + 1) * HEAD)
            total = None
            for skip in range(0, count, most):
                lanes = min(most, count - skip)
                span = lanes * hist_rows
                keys = kv[layer, pl.ds(first + skip, lanes), :, cols].reshape(span, HEAD)
                here = pl.ds(pl.multiple_of((first + skip) * hist_rows, hist_rows), span)
                part = jnp.dot(
                    weigh(queries[rows, cols], keys), live_values[here, cols],
                    preferred_element_type=f32,
                )
                total = part if total is None else total + part
            if more:
                total = summed[rows, cols] + total
            summed[rows, cols] = total

    def finish(layer, start, rows):
        here = rows_of(start)
        hidden = (normalize(summed[here, :]) * gate[here, :]).astype(bf16)
        return (
            rows.astype(f32)
            + jnp.dot(hidden, w_out_ref[layer], preferred_element_type=f32)
        ).astype(bf16)

    def pair(rows_ref, chip):
        return rows_ref[pl.ds(2 * chip, 2)].reshape(tile, D)

    def give_back(source, owner, which, peer):
        return pltpu.make_async_remote_copy(
            src_ref=source.at[peer], dst_ref=returned.at[owner], send_sem=back_send.at[which, peer],
            recv_sem=back_recv.at[owner], device_id={"grp": peer}, device_id_type=MESH,
        )

    def send_home(source, owner, which, chip):
        source[pl.ds(2 * chip, 2)] = finish(0, chip * tile, pair(source, chip)).reshape(2, MOST, D)

        @pl.loop(0, 2)
        def _(lane):
            peer = 2 * chip + lane

            @pl.when(peer != me)
            def _():
                give_back(source, owner, which, peer).start()

            @pl.when(peer == me)
            def _():
                returned[owner] = source[peer]

    def home_at(turn):
        return jnp.where(lower, chips - 1 - turn, turn)

    @pl.when(inner)
    def _():
        @pl.loop(0, chips)
        def _(chip):
            project(0, chip * tile, pair(found, chip))

        relay(0, pos + inward)
        attend_in_turn(0, slots, min(slots, 1024))

        relay(1, pos - inward)

        @pl.loop(0, chips)
        def _(turn):
            send_home(found, me, 0, home_at(turn))

    relay(1, pos + inward)

    @pl.loop(0, chips)
    def _(turn):
        @pl.when(helper)
        def _():
            @pl.when(turn % 2 == 0)
            def _():
                handed_over(turn // 2).wait_recv()

            chip = home_at(turn)
            project(0, chip * tile, pair(handed, chip))
            attend_all(0, chip * tile)
            send_home(handed, end_device, 1, chip)

        @pl.when(turn == chips // 2 - 1)
        def _():
            relay(1, pos - 2 * inward)
            relay(1, pos + 2 * inward)

    def owner_at(turn):
        chip = jnp.where(turn < chips - 1, (turn + 1) % (chips - 1), turn)
        return jnp.where(lower, chip, chips - 1 - chip)

    def enter(turn):
        chip = owner_at(turn)
        worker = 2 * jnp.clip(chip, 1, chips - 2)

        @pl.loop(0, 2)
        def _(lane):
            @pl.when(worker + lane != me)
            def _():
                give_back(returned, 2 * chip + lane, 0, worker + lane).wait_recv()

        project(1, turn * tile, pair(returned, chip))

    def leave(turn, fresh=False):
        chip = owner_at(turn)
        rows = finish(1, turn * tile, pair(returned, chip))
        moved = jnp.dot(place[chip], rows, preferred_element_type=f32).astype(bf16)
        out_ref[...] = moved if fresh else out_ref[...] + moved

    last = jnp.where(lower, chips - 1, 0)
    for distance in range(3, chips):
        for chip in (pos - distance * inward, pos + distance * inward):
            @pl.when(chip != last)
            def _():
                relay(1, chip)

    @pl.loop(0, chips - 1)
    def _(k):
        open_values(1, k + jnp.where(lower, 0, 1))

    enter(0)
    attend_all(1, 0, jnp.where(lower, 0, 2), groups - 2)

    @pl.when((last - pos) * inward > 2)
    def _():
        relay(1, last)

    open_values(1, last)
    attend_all(1, 0, 2 * last, 2, more=True)
    leave(0, fresh=True)

    @pl.loop(1, chips)
    def _(turn):
        enter(turn)
        attend_all(1, turn * tile)
        leave(turn)

    for layer in range(LAYERS):
        @pl.loop(0, chips)
        def _(chip):
            for part in range(PARTS):
                @pl.when(goes_right(layer, chip))
                def _():
                    to_right(layer, chip, part).wait_send()

                @pl.when(goes_left(layer, chip))
                def _():
                    to_left(layer, chip, part).wait_send()

                @pl.when(goes_across(layer))
                def _():
                    to_sibling(layer, chip, part).wait_send()

    @pl.loop(1, groups)
    def _(k):
        peer = (me + k) % groups
        ask(peer, peer).wait_send()

        @pl.when(inner)
        def _():
            give_back(found, me, 0, peer).wait_send()

        @pl.when(helper)
        def _():
            give_back(handed, end_device, 1, peer).wait_send()

    @pl.when(jnp.logical_not(inner))
    def _():
        @pl.loop(0, batches)
        def _(turn):
            hand_over(turn).wait_send()


def body(item_table, cand_owner, cand_row, hist_kv, hist_len, w_in, w_out):
    groups = lax.axis_size("grp")
    cands = cand_row.shape[1]
    hist_rows = hist_kv.shape[2]
    vmem = pl.BlockSpec(memory_space=pltpu.VMEM)
    far = pl.BlockSpec(memory_space=pl.ANY)
    dma, f32, bf16 = pltpu.SemaphoreType.DMA, jnp.float32, jnp.bfloat16
    chips = groups // 2
    rows = pl.pallas_call(
        partial(kernel, groups),
        out_shape=jax.ShapeDtypeStruct((cands, D), bf16),
        in_specs=[
            pl.BlockSpec(memory_space=pltpu.SMEM), vmem, vmem, far, far, far, far,
        ],
        out_specs=vmem,
        scratch_shapes=[
            pltpu.VMEM(item_table.shape, bf16),
            pltpu.VMEM(w_in.shape, bf16),
            pltpu.VMEM(w_out.shape, bf16),
            pltpu.VMEM((LAYERS, groups, hist_rows, 2 * D), bf16),
            pltpu.VMEM((groups * hist_rows, D), bf16),
            pltpu.VMEM((chips, cands, 2 * MOST), bf16),
            pltpu.VMEM((groups, 1, MOST), jnp.int32),
            pltpu.VMEM((groups, 1, MOST), jnp.int32),
            pltpu.VMEM((groups, MOST, D), bf16),
            pltpu.VMEM((groups, MOST, D), bf16),
            pltpu.VMEM((groups, MOST, D), bf16),
            pltpu.VMEM((groups * MOST, D), bf16),
            pltpu.VMEM((groups * MOST, D), f32),
            pltpu.VMEM((groups * MOST, D), f32),
            dma((3,)),
            dma((LAYERS,)),
            dma((LAYERS, chips, PARTS)),
            dma((LAYERS, chips, PARTS)),
            dma((LAYERS, chips, PARTS)),
            dma((LAYERS, chips, PARTS)),
            dma((LAYERS, chips, PARTS)),
            dma((groups,)),
            dma((groups,)),
            dma((groups // 4,)),
            dma((groups // 4,)),
            dma((2, groups)),
            dma((groups,)),
        ],
        compiler_params=pltpu.CompilerParams(
            collective_id=0, has_side_effects=True, vmem_limit_bytes=56 * 1024 * 1024
        ),
    )(hist_len, cand_owner[:, :, 0], cand_row, item_table, hist_kv[:, 0], w_in, w_out)
    return rows[None]


def solution(mesh):
    in_specs = (
        P("grp", None),
        P("req", "grp", None),
        P("req", "grp"),
        P(None, "req", "grp", None),
        P("req"),
        P(),
        P(),
    )
    out_specs = P("req", "grp", None)
    return jax.shard_map(body, mesh=mesh, in_specs=in_specs, out_specs=out_specs, check_vma=False)
```

```python
from functools import partial

import jax
import jax.numpy as jnp
from jax import lax
from jax.experimental import pallas as pl
from jax.experimental.pallas import tpu as pltpu
from jax.sharding import PartitionSpec as P

D = 512
HEADS = 4
HEAD = 128
LAYERS = 2
MOST = 128
PARTS = 4
MESH = pl.DeviceIdType.MESH

score_scale = 0.35
epsilon = 1e-05


def normalize(values):
    center = values - jnp.mean(values, axis=-1, keepdims=True)
    return center * lax.rsqrt(jnp.mean(center * center, axis=-1, keepdims=True) + epsilon)


def silu_of_twice(half):
    return half + half * jnp.tanh(half)


def kernel(
    groups,
    len_ref, owner_ref, row_ref, table_hbm, hist_ref, w_in_hbm, w_out_hbm, out_ref,
    table_ref, w_in_ref, w_out_ref, kv, live_values, place, asked, wanted, found, handed, returned, queries, gate, summed,
    load_sem, own_sem, z_recv, s_recv, r_send, l_send, s_send, ask_send, ask_recv,
    hand_send, hand_recv, back_send, back_recv,
):
    chips = groups // 2
    me = lax.axis_index("grp")
    pos, core = me // 2, me % 2
    sibling = 2 * pos + 1 - core
    lower = pos < chips // 2
    inner = jnp.logical_and(pos > 0, pos + 1 < chips)
    helper = jnp.logical_or(pos == 1, pos == chips - 2)
    inward = jnp.where(lower, 1, -1)
    end_device = 2 * jnp.where(lower, 0, chips - 1) + core
    cands = row_ref.shape[1]
    items = table_ref.shape[0]
    hist_rows = hist_ref.shape[1]
    keys_all = groups * hist_rows
    tile = 2 * MOST
    slots = groups * MOST
    half = hist_rows // PARTS
    f32, bf16 = jnp.float32, jnp.bfloat16

    barrier = pltpu.get_barrier_semaphore()

    @pl.loop(1, groups)
    def _(k):
        pl.semaphore_signal(
            barrier, inc=1, device_id={"grp": (me + k) % groups}, device_id_type=MESH
        )

    own_copies = [
        pltpu.make_async_copy(hist_ref.at[layer], kv.at[layer, me], own_sem.at[layer])
        for layer in range(LAYERS)
    ]
    loads = [
        pltpu.make_async_copy(far, near, load_sem.at[index])
        for index, (far, near) in enumerate(
            [(table_hbm, table_ref), (w_in_hbm, w_in_ref), (w_out_hbm, w_out_ref)]
        )
    ]
    for copy in own_copies + loads:
        copy.start()

    def push(layer, chip, lane, part, target, send, recv):
        block = kv.at[layer, 2 * chip + lane, pl.ds(part * half, half)]
        return pltpu.make_async_remote_copy(
            src_ref=block, dst_ref=block, send_sem=send.at[layer, chip, part],
            recv_sem=recv.at[layer, chip, part], device_id={"grp": target}, device_id_type=MESH,
        )

    def to_right(layer, chip, part):
        return push(layer, chip, core, part, me + 2, r_send, z_recv)

    def to_left(layer, chip, part):
        return push(layer, chip, core, part, me - 2, l_send, z_recv)

    def to_sibling(layer, chip, part):
        return push(layer, chip, core, part, sibling, s_send, s_recv)

    def from_sibling(layer, chip, part):
        return push(layer, chip, 1 - core, part, sibling, s_send, s_recv)

    def margin(layer):
        return 1 if layer == 0 else 0

    def goes_right(layer, chip):
        return jnp.logical_and(chip <= pos, pos + 1 < chips - margin(layer))

    def goes_left(layer, chip):
        return jnp.logical_and(chip >= pos, pos > margin(layer))

    def goes_across(layer):
        return inner if layer == 0 else pos >= 0

    def pass_on(layer, chip, inside=True, outside=True, across=True, parts=range(PARTS)):
        for part in parts:
            if inside or outside:
                right = goes_right(layer, chip)
                left = goes_left(layer, chip)
                if not outside:
                    right, left = jnp.logical_and(right, lower), jnp.logical_and(left, jnp.logical_not(lower))
                if not inside:
                    right, left = jnp.logical_and(right, jnp.logical_not(lower)), jnp.logical_and(left, lower)

                @pl.when(right)
                def _():
                    to_right(layer, chip, part).start()

                @pl.when(left)
                def _():
                    to_left(layer, chip, part).start()

            if across:
                @pl.when(goes_across(layer))
                def _():
                    to_sibling(layer, chip, part).start()

    def when_there(chip, act):
        @pl.when(jnp.logical_and(chip >= 0, chip < chips))
        def _():
            act(chip)

    def relay(layer, chip, parts=range(PARTS)):
        def act(chip):
            for part in parts:
                to_right(layer, chip, part).wait_recv()
                pass_on(layer, chip, parts=[part])

        when_there(chip, act)

    owners = jnp.concatenate(
        [
            jnp.broadcast_to(owner_ref[:, start : start + 128].astype(f32), (128, 128)).T[:, 0:1]
            for start in range(0, cands, 128)
        ],
        axis=0,
    ).astype(jnp.int32)
    names = (owners == lax.broadcasted_iota(jnp.int32, (cands, 128), 1)).astype(f32)
    names16 = names.astype(bf16)
    item_rows = row_ref[...]
    high = (item_rows >> 6).astype(f32)
    low = (item_rows & 63).astype(f32)
    halves = jnp.concatenate([high, low, jnp.zeros((6, cands), f32)], axis=0).astype(bf16)
    listed = jnp.zeros((8, slots), f32)
    for start in range(0, cands, tile):
        earlier = (
            lax.broadcasted_iota(jnp.int32, (tile, cands), 1)
            < start + lax.broadcasted_iota(jnp.int32, (tile, cands), 0)
        ).astype(f32).astype(bf16)
        rank = jnp.dot(earlier, names16, preferred_element_type=f32)
        own_rank = jnp.sum(rank * names[start : start + tile], axis=1, keepdims=True)
        flat = owners[start : start + tile] * MOST + own_rank.astype(jnp.int32)
        chosen = (
            (flat == lax.broadcasted_iota(jnp.int32, (tile, slots), 1)).astype(f32).astype(bf16)
        )
        listed += jnp.dot(halves[:, start : start + tile], chosen, preferred_element_type=f32)
        for chip in range(chips):
            place[chip, start : start + tile, :] = chosen[:, chip * tile : (chip + 1) * tile]
    requested = (listed[0:1] * 64.0 + listed[1:2]).astype(jnp.int32)
    for owner in range(groups):
        asked[owner] = requested[:, owner * MOST : (owner + 1) * MOST]

    pl.semaphore_wait(barrier, groups - 1)

    def ask(peer, slot):
        return pltpu.make_async_remote_copy(
            src_ref=asked.at[peer], dst_ref=wanted.at[slot], send_sem=ask_send.at[peer],
            recv_sem=ask_recv.at[slot], device_id={"grp": peer}, device_id_type=MESH,
        )

    @pl.loop(1, groups)
    def _(k):
        ask((me + k) % groups, me).start()

    own_copies[0].wait()
    pass_on(0, pos)
    own_copies[1].wait()

    @pl.when(inner)
    def _():
        pass_on(1, pos, inside=False)

    @pl.when(jnp.logical_not(inner))
    def _():
        pass_on(1, pos)

    wanted[me] = asked[me]

    @pl.loop(1, groups)
    def _(k):
        peer = (me + k) % groups
        ask(peer, peer).wait_recv()

    early, late = range(PARTS // 2), range(PARTS // 2, PARTS)

    @pl.when(inner)
    def _():
        pass_on(1, pos, outside=False, across=False)
        relay(0, pos - inward, early)

    at_once = 4
    chunk = 512
    batches = groups // at_once

    def batch_at(turn):
        return jnp.where(lower, batches - 1 - turn, turn)

    def hand_over(turn):
        block = pl.ds(batch_at(turn) * at_once, at_once)
        target = 2 * jnp.clip(pos, 1, chips - 2) + core
        return pltpu.make_async_remote_copy(
            src_ref=found.at[block], dst_ref=handed.at[block], send_sem=hand_send.at[turn],
            recv_sem=hand_recv.at[turn], device_id={"grp": target}, device_id_type=MESH,
        )

    def handed_over(turn):
        block = pl.ds(batch_at(turn) * at_once, at_once)
        return pltpu.make_async_remote_copy(
            src_ref=found.at[block], dst_ref=handed.at[block], send_sem=hand_send.at[turn],
            recv_sem=hand_recv.at[turn], device_id={"grp": end_device}, device_id_type=MESH,
        )

    def gather(turn):
        batch = batch_at(turn)
        columns = []
        for k in range(at_once):
            line = wanted[batch * at_once + k].astype(f32)
            columns.append(jnp.broadcast_to(line, (MOST, MOST)).T[:, 0:1].astype(jnp.int32))
        column = jnp.concatenate(columns, axis=0)
        total = jnp.zeros((at_once * MOST, D), f32)
        for start in range(0, items, chunk):
            picks = (
                column
                == start + lax.broadcasted_iota(jnp.int32, (at_once * MOST, chunk), 1)
            ).astype(f32).astype(bf16)
            total += jnp.dot(
                picks, table_ref[start : start + chunk, :], preferred_element_type=f32
            )
        found[pl.ds(batch * at_once, at_once)] = total.astype(bf16).reshape(at_once, MOST, D)

        @pl.when(jnp.logical_not(inner))
        def _():
            hand_over(turn).start()

        @pl.when(jnp.logical_and(inner, turn == 0))
        def _():
            relay(0, pos - inward, late)

    loads[0].wait()
    pl.loop(0, batches)(gather)
    loads[1].wait()
    loads[2].wait()

    def rows_of(start, size=tile):
        return pl.ds(pl.multiple_of(start, tile), size)

    def project(layer, start, rows):
        normed = normalize(rows.astype(f32)).astype(bf16)
        projected = silu_of_twice(
            0.5 * jnp.dot(normed, w_in_ref[layer], preferred_element_type=f32)
        )
        gate[rows_of(start), :] = projected[:, :D]
        queries[rows_of(start), :] = projected[:, D:].astype(bf16)
        summed[rows_of(start), :] = jnp.zeros((tile, D), f32)

    length = len_ref[0]

    def open_values(layer, chip):
        for part in range(PARTS):
            from_sibling(layer, chip, part).wait_recv()
        for lane in range(2):
            first = (2 * chip + lane) * hist_rows
            position = first + lax.broadcasted_iota(jnp.int32, (hist_rows, D), 0)
            values = kv[layer, 2 * chip + lane, :, D:].astype(f32)
            live_values[pl.ds(pl.multiple_of(first, hist_rows), hist_rows), :] = jnp.where(
                position < length, values, 0.0
            ).astype(bf16)

    def weigh(asking, keys):
        scores = lax.dot_general(
            asking, keys, (((1,), (1,)), ((), ())), preferred_element_type=f32
        )
        return silu_of_twice((scores * (0.5 * score_scale)).astype(bf16))

    def attend(layer, chip, size, block):
        open_values(layer, chip)
        here = pl.ds(pl.multiple_of(2 * chip * hist_rows, 2 * hist_rows), 2 * hist_rows)

        @pl.loop(0, size // block)
        def _(step):
            rows = rows_of(step * block, block)
            for head in range(HEADS):
                cols = slice(head * HEAD, (head + 1) * HEAD)
                keys = kv[layer, pl.ds(2 * chip, 2), :, cols].reshape(2 * hist_rows, HEAD)
                summed[rows, cols] += jnp.dot(
                    weigh(queries[rows, cols], keys), live_values[here, cols],
                    preferred_element_type=f32,
                )

    def attend_in_turn(layer, size, block):
        @pl.loop(0, 2 * chips - 1)
        def _(turn):
            distance = (turn + 1) // 2
            chip = pos + inward * jnp.where(turn % 2 == 0, distance, -distance)

            @pl.when(distance > 1)
            def _():
                relay(layer, chip)

            when_there(chip, lambda chip: attend(layer, chip, size, block))

    def attend_all(layer, start, first=0, count=groups, more=False):
        rows = rows_of(start)
        most = max(1, 2048 // hist_rows)
        for head in range(HEADS):
            cols = slice(head * HEAD, (head + 1) * HEAD)
            total = None
            for skip in range(0, count, most):
                lanes = min(most, count - skip)
                span = lanes * hist_rows
                keys = kv[layer, pl.ds(first + skip, lanes), :, cols].reshape(span, HEAD)
                here = pl.ds(pl.multiple_of((first + skip) * hist_rows, hist_rows), span)
                part = jnp.dot(
                    weigh(queries[rows, cols], keys), live_values[here, cols],
                    preferred_element_type=f32,
                )
                total = part if total is None else total + part
            if more:
                total = summed[rows, cols] + total
            summed[rows, cols] = total

    def finish(layer, start, rows):
        here = rows_of(start)
        hidden = (normalize(summed[here, :]) * gate[here, :]).astype(bf16)
        return (
            rows.astype(f32)
            + jnp.dot(hidden, w_out_ref[layer], preferred_element_type=f32)
        ).astype(bf16)

    def pair(rows_ref, chip):
        return rows_ref[pl.ds(2 * chip, 2)].reshape(tile, D)

    def give_back(source, owner, which, peer):
        return pltpu.make_async_remote_copy(
            src_ref=source.at[peer], dst_ref=returned.at[owner], send_sem=back_send.at[which, peer],
            recv_sem=back_recv.at[owner], device_id={"grp": peer}, device_id_type=MESH,
        )

    def send_home(source, owner, which, chip):
        source[pl.ds(2 * chip, 2)] = finish(0, chip * tile, pair(source, chip)).reshape(2, MOST, D)

        @pl.loop(0, 2)
        def _(lane):
            peer = 2 * chip + lane

            @pl.when(peer != me)
            def _():
                give_back(source, owner, which, peer).start()

            @pl.when(peer == me)
            def _():
                returned[owner] = source[peer]

    def home_at(turn):
        return jnp.where(lower, chips - 1 - turn, turn)

    @pl.when(inner)
    def _():
        @pl.loop(0, chips)
        def _(chip):
            project(0, chip * tile, pair(found, chip))

        relay(0, pos + inward)
        relay(1, pos + inward)
        attend_in_turn(0, slots, min(slots, 1024))

        relay(1, pos - inward)

        @pl.loop(0, chips)
        def _(turn):
            send_home(found, me, 0, home_at(chips - 1 - turn))

    @pl.when(jnp.logical_not(inner))
    def _():
        relay(1, pos + inward)

    @pl.loop(0, chips)
    def _(turn):
        @pl.when(helper)
        def _():
            @pl.when(turn % 2 == 0)
            def _():
                handed_over(turn // 2).wait_recv()

            chip = home_at(turn)
            project(0, chip * tile, pair(handed, chip))
            attend_all(0, chip * tile)
            send_home(handed, end_device, 1, chip)

        for parts, when in ((early, chips // 2 - 2), (late, chips // 2 - 1)):
            @pl.when(turn == when)
            def _():
                relay(1, pos - 2 * inward, parts)
                relay(1, pos + 2 * inward, parts)

    def owner_at(turn):
        chip = jnp.where(turn < chips - 1, (turn + 1) % (chips - 1), turn)
        return jnp.where(lower, chip, chips - 1 - chip)

    def enter(turn):
        chip = owner_at(turn)
        worker = 2 * jnp.clip(chip, 1, chips - 2)

        @pl.loop(0, 2)
        def _(lane):
            @pl.when(worker + lane != me)
            def _():
                give_back(returned, 2 * chip + lane, 0, worker + lane).wait_recv()

        project(1, turn * tile, pair(returned, chip))

    def leave(turn, fresh=False):
        chip = owner_at(turn)
        rows = finish(1, turn * tile, pair(returned, chip))
        moved = jnp.dot(place[chip], rows, preferred_element_type=f32).astype(bf16)
        out_ref[...] = moved if fresh else out_ref[...] + moved

    last = jnp.where(lower, chips - 1, 0)
    for distance in range(3, chips):
        for chip in (pos - distance * inward, pos + distance * inward):
            @pl.when(chip != last)
            def _():
                relay(1, chip)

    @pl.loop(0, chips - 1)
    def _(k):
        open_values(1, k + jnp.where(lower, 0, 1))

    ready = chips // 2

    @pl.loop(0, ready)
    def _(turn):
        enter(turn)
        attend_all(1, turn * tile, jnp.where(lower, 0, 2), groups - 2)

    @pl.when((last - pos) * inward > 2)
    def _():
        relay(1, last)

    attend(1, last, ready * tile, ready * tile)
    leave(0, fresh=True)
    pl.loop(1, ready)(leave)

    @pl.loop(ready, chips)
    def _(turn):
        enter(turn)
        attend_all(1, turn * tile)
        leave(turn)

    for layer in range(LAYERS):
        @pl.loop(0, chips)
        def _(chip):
            for part in range(PARTS):
                @pl.when(goes_right(layer, chip))
                def _():
                    to_right(layer, chip, part).wait_send()

                @pl.when(goes_left(layer, chip))
                def _():
                    to_left(layer, chip, part).wait_send()

                @pl.when(goes_across(layer))
                def _():
                    to_sibling(layer, chip, part).wait_send()

    @pl.loop(1, groups)
    def _(k):
        peer = (me + k) % groups
        ask(peer, peer).wait_send()

        @pl.when(inner)
        def _():
            give_back(found, me, 0, peer).wait_send()

        @pl.when(helper)
        def _():
            give_back(handed, end_device, 1, peer).wait_send()

    @pl.when(jnp.logical_not(inner))
    def _():
        @pl.loop(0, batches)
        def _(turn):
            hand_over(turn).wait_send()


def body(item_table, cand_owner, cand_row, hist_kv, hist_len, w_in, w_out):
    groups = lax.axis_size("grp")
    cands = cand_row.shape[1]
    hist_rows = hist_kv.shape[2]
    vmem = pl.BlockSpec(memory_space=pltpu.VMEM)
    far = pl.BlockSpec(memory_space=pl.ANY)
    dma, f32, bf16 = pltpu.SemaphoreType.DMA, jnp.float32, jnp.bfloat16
    chips = groups // 2
    rows = pl.pallas_call(
        partial(kernel, groups),
        out_shape=jax.ShapeDtypeStruct((cands, D), bf16),
        in_specs=[
            pl.BlockSpec(memory_space=pltpu.SMEM), vmem, vmem, far, far, far, far,
        ],
        out_specs=vmem,
        scratch_shapes=[
            pltpu.VMEM(item_table.shape, bf16),
            pltpu.VMEM(w_in.shape, bf16),
            pltpu.VMEM(w_out.shape, bf16),
            pltpu.VMEM((LAYERS, groups, hist_rows, 2 * D), bf16),
            pltpu.VMEM((groups * hist_rows, D), bf16),
            pltpu.VMEM((chips, cands, 2 * MOST), bf16),
            pltpu.VMEM((groups, 1, MOST), jnp.int32),
            pltpu.VMEM((groups, 1, MOST), jnp.int32),
            pltpu.VMEM((groups, MOST, D), bf16),
            pltpu.VMEM((groups, MOST, D), bf16),
            pltpu.VMEM((groups, MOST, D), bf16),
            pltpu.VMEM((groups * MOST, D), bf16),
            pltpu.VMEM((groups * MOST, D), f32),
            pltpu.VMEM((groups * MOST, D), f32),
            dma((3,)),
            dma((LAYERS,)),
            dma((LAYERS, chips, PARTS)),
            dma((LAYERS, chips, PARTS)),
            dma((LAYERS, chips, PARTS)),
            dma((LAYERS, chips, PARTS)),
            dma((LAYERS, chips, PARTS)),
            dma((groups,)),
            dma((groups,)),
            dma((groups // 4,)),
            dma((groups // 4,)),
            dma((2, groups)),
            dma((groups,)),
        ],
        compiler_params=pltpu.CompilerParams(
            collective_id=0, has_side_effects=True, vmem_limit_bytes=56 * 1024 * 1024
        ),
    )(hist_len, cand_owner[:, :, 0], cand_row, item_table, hist_kv[:, 0], w_in, w_out)
    return rows[None]


def solution(mesh):
    in_specs = (
        P("grp", None),
        P("req", "grp", None),
        P("req", "grp"),
        P(None, "req", "grp", None),
        P("req"),
        P(),
        P(),
    )
    out_specs = P("req", "grp", None)
    return jax.shard_map(body, mesh=mesh, in_specs=in_specs, out_specs=out_specs, check_vma=False)
```

```python
from functools import partial

import jax
import jax.numpy as jnp
from jax import lax
from jax.experimental import pallas as pl
from jax.experimental.pallas import tpu as pltpu
from jax.sharding import PartitionSpec as P

D = 512
HEADS = 4
HEAD = 128
LAYERS = 2
MOST = 128
PARTS = 4
MESH = pl.DeviceIdType.MESH

score_scale = 0.35
epsilon = 1e-05


def normalize(values):
    center = values - jnp.mean(values, axis=-1, keepdims=True)
    return center * lax.rsqrt(jnp.mean(center * center, axis=-1, keepdims=True) + epsilon)


def silu_of_twice(half):
    return half + half * jnp.tanh(half)


def kernel(
    groups,
    len_ref, owner_ref, row_ref, table_hbm, hist_ref, w_in_hbm, w_out_hbm, out_ref,
    table_ref, w_in_ref, w_out_ref, kv, live_values, place, asked, wanted, found, handed, returned, queries, gate, summed,
    load_sem, own_sem, z_recv, s_recv, r_send, l_send, s_send, ask_send, ask_recv,
    hand_send, hand_recv, back_send, back_recv,
):
    chips = groups // 2
    me = lax.axis_index("grp")
    pos, core = me // 2, me % 2
    sibling = 2 * pos + 1 - core
    lower = pos < chips // 2
    inner = jnp.logical_and(pos > 0, pos + 1 < chips)
    helper = jnp.logical_or(pos == 1, pos == chips - 2)
    inward = jnp.where(lower, 1, -1)
    end_device = 2 * jnp.where(lower, 0, chips - 1) + core
    cands = row_ref.shape[1]
    items = table_ref.shape[0]
    hist_rows = hist_ref.shape[1]
    keys_all = groups * hist_rows
    tile = 2 * MOST
    slots = groups * MOST
    half = hist_rows // PARTS
    f32, bf16 = jnp.float32, jnp.bfloat16

    barrier = pltpu.get_barrier_semaphore()

    @pl.loop(1, groups)
    def _(k):
        pl.semaphore_signal(
            barrier, inc=1, device_id={"grp": (me + k) % groups}, device_id_type=MESH
        )

    own_copies = [
        pltpu.make_async_copy(hist_ref.at[layer], kv.at[layer, me], own_sem.at[layer])
        for layer in range(LAYERS)
    ]
    loads = [
        pltpu.make_async_copy(far, near, load_sem.at[index])
        for index, (far, near) in enumerate(
            [(table_hbm, table_ref), (w_in_hbm, w_in_ref), (w_out_hbm, w_out_ref)]
        )
    ]
    for copy in own_copies + loads:
        copy.start()

    def push(layer, chip, lane, part, target, send, recv):
        block = kv.at[layer, 2 * chip + lane, pl.ds(part * half, half)]
        return pltpu.make_async_remote_copy(
            src_ref=block, dst_ref=block, send_sem=send.at[layer, chip, part],
            recv_sem=recv.at[layer, chip, part], device_id={"grp": target}, device_id_type=MESH,
        )

    def to_right(layer, chip, part):
        return push(layer, chip, core, part, me + 2, r_send, z_recv)

    def to_left(layer, chip, part):
        return push(layer, chip, core, part, me - 2, l_send, z_recv)

    def to_sibling(layer, chip, part):
        return push(layer, chip, core, part, sibling, s_send, s_recv)

    def from_sibling(layer, chip, part):
        return push(layer, chip, 1 - core, part, sibling, s_send, s_recv)

    def margin(layer):
        return 1 if layer == 0 else 0

    def goes_right(layer, chip):
        return jnp.logical_and(chip <= pos, pos + 1 < chips - margin(layer))

    def goes_left(layer, chip):
        return jnp.logical_and(chip >= pos, pos > margin(layer))

    def goes_across(layer):
        return inner if layer == 0 else pos >= 0

    def pass_on(layer, chip, inside=True, outside=True, across=True, parts=range(PARTS)):
        for part in parts:
            if inside or outside:
                right = goes_right(layer, chip)
                left = goes_left(layer, chip)
                if not outside:
                    right, left = jnp.logical_and(right, lower), jnp.logical_and(left, jnp.logical_not(lower))
                if not inside:
                    right, left = jnp.logical_and(right, jnp.logical_not(lower)), jnp.logical_and(left, lower)

                @pl.when(right)
                def _():
                    to_right(layer, chip, part).start()

                @pl.when(left)
                def _():
                    to_left(layer, chip, part).start()

            if across:
                @pl.when(goes_across(layer))
                def _():
                    to_sibling(layer, chip, part).start()

    def when_there(chip, act):
        @pl.when(jnp.logical_and(chip >= 0, chip < chips))
        def _():
            act(chip)

    def relay(layer, chip, parts=range(PARTS)):
        def act(chip):
            for part in parts:
                to_right(layer, chip, part).wait_recv()
                pass_on(layer, chip, parts=[part])

        when_there(chip, act)

    owners = jnp.concatenate(
        [
            jnp.broadcast_to(owner_ref[:, start : start + 128].astype(f32), (128, 128)).T[:, 0:1]
            for start in range(0, cands, 128)
        ],
        axis=0,
    ).astype(jnp.int32)
    names = (owners == lax.broadcasted_iota(jnp.int32, (cands, 128), 1)).astype(f32)
    names16 = names.astype(bf16)
    item_rows = row_ref[...]
    high = (item_rows >> 6).astype(f32)
    low = (item_rows & 63).astype(f32)
    halves = jnp.concatenate([high, low, jnp.zeros((6, cands), f32)], axis=0).astype(bf16)
    listed = jnp.zeros((8, slots), f32)
    for start in range(0, cands, tile):
        earlier = (
            lax.broadcasted_iota(jnp.int32, (tile, cands), 1)
            < start + lax.broadcasted_iota(jnp.int32, (tile, cands), 0)
        ).astype(f32).astype(bf16)
        rank = jnp.dot(earlier, names16, preferred_element_type=f32)
        own_rank = jnp.sum(rank * names[start : start + tile], axis=1, keepdims=True)
        flat = owners[start : start + tile] * MOST + own_rank.astype(jnp.int32)
        chosen = (
            (flat == lax.broadcasted_iota(jnp.int32, (tile, slots), 1)).astype(f32).astype(bf16)
        )
        listed += jnp.dot(halves[:, start : start + tile], chosen, preferred_element_type=f32)
        for chip in range(chips):
            place[chip, start : start + tile, :] = chosen[:, chip * tile : (chip + 1) * tile]
    requested = (listed[0:1] * 64.0 + listed[1:2]).astype(jnp.int32)
    for owner in range(groups):
        asked[owner] = requested[:, owner * MOST : (owner + 1) * MOST]

    pl.semaphore_wait(barrier, groups - 1)

    def ask(peer, slot):
        return pltpu.make_async_remote_copy(
            src_ref=asked.at[peer], dst_ref=wanted.at[slot], send_sem=ask_send.at[peer],
            recv_sem=ask_recv.at[slot], device_id={"grp": peer}, device_id_type=MESH,
        )

    @pl.loop(1, groups)
    def _(k):
        ask((me + k) % groups, me).start()

    own_copies[0].wait()
    pass_on(0, pos)
    own_copies[1].wait()

    @pl.when(inner)
    def _():
        pass_on(1, pos, inside=False)

    @pl.when(jnp.logical_not(inner))
    def _():
        pass_on(1, pos)

    wanted[me] = asked[me]

    @pl.loop(1, groups)
    def _(k):
        peer = (me + k) % groups
        ask(peer, peer).wait_recv()

    early, late = range(PARTS // 2), range(PARTS // 2, PARTS)

    @pl.when(inner)
    def _():
        pass_on(1, pos, outside=False, across=False)
        relay(0, pos - inward, early)

    at_once = 4
    chunk = 512
    batches = groups // at_once

    def batch_at(turn):
        return jnp.where(lower, batches - 1 - turn, turn)

    def hand_over(turn):
        block = pl.ds(batch_at(turn) * at_once, at_once)
        target = 2 * jnp.clip(pos, 1, chips - 2) + core
        return pltpu.make_async_remote_copy(
            src_ref=found.at[block], dst_ref=handed.at[block], send_sem=hand_send.at[turn],
            recv_sem=hand_recv.at[turn], device_id={"grp": target}, device_id_type=MESH,
        )

    def handed_over(turn):
        block = pl.ds(batch_at(turn) * at_once, at_once)
        return pltpu.make_async_remote_copy(
            src_ref=found.at[block], dst_ref=handed.at[block], send_sem=hand_send.at[turn],
            recv_sem=hand_recv.at[turn], device_id={"grp": end_device}, device_id_type=MESH,
        )

    def gather(turn):
        batch = batch_at(turn)
        columns = []
        for k in range(at_once):
            line = wanted[batch * at_once + k].astype(f32)
            columns.append(jnp.broadcast_to(line, (MOST, MOST)).T[:, 0:1].astype(jnp.int32))
        column = jnp.concatenate(columns, axis=0)
        total = jnp.zeros((at_once * MOST, D), f32)
        for start in range(0, items, chunk):
            picks = (
                column
                == start + lax.broadcasted_iota(jnp.int32, (at_once * MOST, chunk), 1)
            ).astype(f32).astype(bf16)
            total += jnp.dot(
                picks, table_ref[start : start + chunk, :], preferred_element_type=f32
            )
        found[pl.ds(batch * at_once, at_once)] = total.astype(bf16).reshape(at_once, MOST, D)

        @pl.when(jnp.logical_not(inner))
        def _():
            hand_over(turn).start()

        @pl.when(jnp.logical_and(inner, turn == 0))
        def _():
            relay(0, pos - inward, late)

    loads[0].wait()
    pl.loop(0, batches)(gather)
    loads[1].wait()
    loads[2].wait()

    def rows_of(start, size=tile):
        return pl.ds(pl.multiple_of(start, tile), size)

    def project(layer, start, rows):
        normed = normalize(rows.astype(f32)).astype(bf16)
        projected = silu_of_twice(
            0.5 * jnp.dot(normed, w_in_ref[layer], preferred_element_type=f32)
        )
        gate[rows_of(start), :] = projected[:, :D]
        queries[rows_of(start), :] = projected[:, D:].astype(bf16)

    length = len_ref[0]

    def open_values(layer, chip):
        for part in range(PARTS):
            from_sibling(layer, chip, part).wait_recv()
        for lane in range(2):
            first = (2 * chip + lane) * hist_rows
            position = first + lax.broadcasted_iota(jnp.int32, (hist_rows, D), 0)
            values = kv[layer, 2 * chip + lane, :, D:].astype(f32)
            live_values[pl.ds(pl.multiple_of(first, hist_rows), hist_rows), :] = jnp.where(
                position < length, values, 0.0
            ).astype(bf16)

    def weigh(asking, keys):
        scores = lax.dot_general(
            asking, keys, (((1,), (1,)), ((), ())), preferred_element_type=f32
        )
        return silu_of_twice((scores * (0.5 * score_scale)).astype(bf16))

    def attend(layer, chip, size, block):
        open_values(layer, chip)
        here = pl.ds(pl.multiple_of(2 * chip * hist_rows, 2 * hist_rows), 2 * hist_rows)

        @pl.loop(0, size // block)
        def _(step):
            rows = rows_of(step * block, block)
            for head in range(HEADS):
                cols = slice(head * HEAD, (head + 1) * HEAD)
                keys = kv[layer, pl.ds(2 * chip, 2), :, cols].reshape(2 * hist_rows, HEAD)
                summed[rows, cols] += jnp.dot(
                    weigh(queries[rows, cols], keys), live_values[here, cols],
                    preferred_element_type=f32,
                )

    def attend_in_turn(layer, size, block):
        @pl.loop(0, 2 * chips - 1)
        def _(turn):
            distance = (turn + 1) // 2
            chip = pos + inward * jnp.where(turn % 2 == 0, distance, -distance)

            @pl.when(distance > 1)
            def _():
                relay(layer, chip)

            when_there(chip, lambda chip: attend(layer, chip, size, block))

    def attend_all(layer, start, first=0, count=groups, more=False):
        rows = rows_of(start)
        most = max(1, 2048 // hist_rows)
        for head in range(HEADS):
            cols = slice(head * HEAD, (head + 1) * HEAD)
            total = None
            for skip in range(0, count, most):
                lanes = min(most, count - skip)
                span = lanes * hist_rows
                keys = kv[layer, pl.ds(first + skip, lanes), :, cols].reshape(span, HEAD)
                here = pl.ds(pl.multiple_of((first + skip) * hist_rows, hist_rows), span)
                part = jnp.dot(
                    weigh(queries[rows, cols], keys), live_values[here, cols],
                    preferred_element_type=f32,
                )
                total = part if total is None else total + part
            if more:
                total = summed[rows, cols] + total
            summed[rows, cols] = total

    def finish(layer, start, rows):
        here = rows_of(start)
        hidden = (normalize(summed[here, :]) * gate[here, :]).astype(bf16)
        return (
            rows.astype(f32)
            + jnp.dot(hidden, w_out_ref[layer], preferred_element_type=f32)
        ).astype(bf16)

    def pair(rows_ref, chip):
        return rows_ref[pl.ds(2 * chip, 2)].reshape(tile, D)

    def give_back(source, owner, which, peer):
        return pltpu.make_async_remote_copy(
            src_ref=source.at[peer], dst_ref=returned.at[owner], send_sem=back_send.at[which, peer],
            recv_sem=back_recv.at[owner], device_id={"grp": peer}, device_id_type=MESH,
        )

    def send_home(source, owner, which, chip):
        source[pl.ds(2 * chip, 2)] = finish(0, chip * tile, pair(source, chip)).reshape(2, MOST, D)

        @pl.loop(0, 2)
        def _(lane):
            peer = 2 * chip + lane

            @pl.when(peer != me)
            def _():
                give_back(source, owner, which, peer).start()

            @pl.when(peer == me)
            def _():
                returned[owner] = source[peer]

    def home_at(turn):
        return jnp.where(lower, chips - 1 - turn, turn)

    @pl.when(inner)
    def _():
        @pl.loop(0, chips)
        def _(chip):
            project(0, chip * tile, pair(found, chip))
            summed[rows_of(chip * tile), :] = jnp.zeros((tile, D), f32)

        relay(0, pos + inward)
        relay(1, pos + inward)
        attend_in_turn(0, slots, min(slots, 1024))

        relay(1, pos - inward)

        @pl.loop(0, chips)
        def _(turn):
            send_home(found, me, 0, home_at(chips - 1 - turn))

    @pl.when(jnp.logical_not(inner))
    def _():
        relay(1, pos + inward)

    @pl.loop(0, chips)
    def _(turn):
        @pl.when(helper)
        def _():
            @pl.when(turn % 2 == 0)
            def _():
                handed_over(turn // 2).wait_recv()

            chip = home_at(jnp.where(turn < chips // 2, turn, turn + 1 - 2 * (turn % 2)))
            project(0, chip * tile, pair(handed, chip))
            attend_all(0, chip * tile)
            send_home(handed, end_device, 1, chip)

        for parts, when in ((early, chips // 2 - 2), (late, chips // 2 - 1)):
            @pl.when(turn == when)
            def _():
                relay(1, pos - 2 * inward, parts)
                relay(1, pos + 2 * inward, parts)

    def owner_at(turn):
        chip = jnp.where(turn < chips - 1, (turn + 1) % (chips - 1), turn)
        return jnp.where(lower, chip, chips - 1 - chip)

    def enter(turn):
        chip = owner_at(turn)
        worker = 2 * jnp.clip(chip, 1, chips - 2)

        @pl.loop(0, 2)
        def _(lane):
            @pl.when(worker + lane != me)
            def _():
                give_back(returned, 2 * chip + lane, 0, worker + lane).wait_recv()

        project(1, turn * tile, pair(returned, chip))

    def leave(turn, fresh=False):
        chip = owner_at(turn)
        rows = finish(1, turn * tile, pair(returned, chip))
        moved = jnp.dot(place[chip], rows, preferred_element_type=f32).astype(bf16)
        out_ref[...] = moved if fresh else out_ref[...] + moved

    last = jnp.where(lower, chips - 1, 0)
    for distance in range(3, chips):
        for chip in (pos - distance * inward, pos + distance * inward):
            @pl.when(chip != last)
            def _():
                relay(1, chip)

    @pl.loop(0, chips - 1)
    def _(k):
        open_values(1, k + jnp.where(lower, 0, 1))

    ready = chips // 2

    @pl.loop(0, ready)
    def _(turn):
        enter(turn)
        attend_all(1, turn * tile, jnp.where(lower, 0, 2), groups - 2)

    @pl.when((last - pos) * inward > 2)
    def _():
        relay(1, last)

    attend(1, last, ready * tile, ready * tile)
    leave(0, fresh=True)
    pl.loop(1, ready)(leave)

    @pl.loop(ready, chips)
    def _(turn):
        enter(turn)
        attend_all(1, turn * tile)
        leave(turn)

    for layer in range(LAYERS):
        @pl.loop(0, chips)
        def _(chip):
            for part in range(PARTS):
                @pl.when(goes_right(layer, chip))
                def _():
                    to_right(layer, chip, part).wait_send()

                @pl.when(goes_left(layer, chip))
                def _():
                    to_left(layer, chip, part).wait_send()

                @pl.when(goes_across(layer))
                def _():
                    to_sibling(layer, chip, part).wait_send()

    @pl.loop(1, groups)
    def _(k):
        peer = (me + k) % groups
        ask(peer, peer).wait_send()

        @pl.when(inner)
        def _():
            give_back(found, me, 0, peer).wait_send()

        @pl.when(helper)
        def _():
            give_back(handed, end_device, 1, peer).wait_send()

    @pl.when(jnp.logical_not(inner))
    def _():
        @pl.loop(0, batches)
        def _(turn):
            hand_over(turn).wait_send()


def body(item_table, cand_owner, cand_row, hist_kv, hist_len, w_in, w_out):
    groups = lax.axis_size("grp")
    cands = cand_row.shape[1]
    hist_rows = hist_kv.shape[2]
    vmem = pl.BlockSpec(memory_space=pltpu.VMEM)
    far = pl.BlockSpec(memory_space=pl.ANY)
    dma, f32, bf16 = pltpu.SemaphoreType.DMA, jnp.float32, jnp.bfloat16
    chips = groups // 2
    rows = pl.pallas_call(
        partial(kernel, groups),
        out_shape=jax.ShapeDtypeStruct((cands, D), bf16),
        in_specs=[
            pl.BlockSpec(memory_space=pltpu.SMEM), vmem, vmem, far, far, far, far,
        ],
        out_specs=vmem,
        scratch_shapes=[
            pltpu.VMEM(item_table.shape, bf16),
            pltpu.VMEM(w_in.shape, bf16),
            pltpu.VMEM(w_out.shape, bf16),
            pltpu.VMEM((LAYERS, groups, hist_rows, 2 * D), bf16),
            pltpu.VMEM((groups * hist_rows, D), bf16),
            pltpu.VMEM((chips, cands, 2 * MOST), bf16),
            pltpu.VMEM((groups, 1, MOST), jnp.int32),
            pltpu.VMEM((groups, 1, MOST), jnp.int32),
            pltpu.VMEM((groups, MOST, D), bf16),
            pltpu.VMEM((groups, MOST, D), bf16),
            pltpu.VMEM((groups, MOST, D), bf16),
            pltpu.VMEM((groups * MOST, D), bf16),
            pltpu.VMEM((groups * MOST, D), f32),
            pltpu.VMEM((groups * MOST, D), f32),
            dma((3,)),
            dma((LAYERS,)),
            dma((LAYERS, chips, PARTS)),
            dma((LAYERS, chips, PARTS)),
            dma((LAYERS, chips, PARTS)),
            dma((LAYERS, chips, PARTS)),
            dma((LAYERS, chips, PARTS)),
            dma((groups,)),
            dma((groups,)),
            dma((groups // 4,)),
            dma((groups // 4,)),
            dma((2, groups)),
            dma((groups,)),
        ],
        compiler_params=pltpu.CompilerParams(
            collective_id=0, has_side_effects=True, vmem_limit_bytes=56 * 1024 * 1024
        ),
    )(hist_len, cand_owner[:, :, 0], cand_row, item_table, hist_kv[:, 0], w_in, w_out)
    return rows[None]


def solution(mesh):
    in_specs = (
        P("grp", None),
        P("req", "grp", None),
        P("req", "grp"),
        P(None, "req", "grp", None),
        P("req"),
        P(),
        P(),
    )
    out_specs = P("req", "grp", None)
    return jax.shard_map(body, mesh=mesh, in_specs=in_specs, out_specs=out_specs, check_vma=False)
```
